256 devices in a mesh: grp: 8 (over y, core), dev: 32 (over z, x).
Axes of the slice: x: 4, y: 4, z: 8, core: 2. Of those that a mesh axis runs over, the one named last changes fastest.
Arguments:
- item_factors: bfloat16 [65536, 256], P(('grp', 'dev'))
- send_list: int32 [256, 8, 1], P(('grp', 'dev')), may hold values from 0 to 1
- route_list: int32 [256, 32, 1], P(('grp', 'dev')), may hold values from 0 to 7
- tile_slot: int32 [256, 64], P(('grp', 'dev')), may hold values from 0 to 31
- confidence: bfloat16 [16384, 128, 128], P(('grp', 'dev')), may hold values from 0 to 160, as said below
Outputs:
- user_factors: float32 [131072, 256], P(('grp', 'dev'))
The draws below stay inside these ranges and needn't reach their ends.
Inputs may be any that keep to these rules, and one draw needn't show every extreme that they name: `confidence`: every user row of every tile has at least one observed item.
All inputs are finite; a program needn't handle non-finite values.
Results may differ from the reference program's by a relative error of at most 0.0055.
Values may be sent and summed in bfloat16 or wider, within the bound.
A program may use at most 128 MiB of HBM per device.

```python
import math
import jax
import jax.numpy as jnp
from jax import lax

RANK = 256
BLOCK = 128
PANELS_DEV = 2
SENT = 1
PICKED = 1
USER_BLOCKS = 4
TILES_PER = 16
ITERS = 8
TILES = 64
ALL_TILES = 16384
USERS = 131072
ITEMS = 65536
N_GRP = 8
N_DEV = 32


def draw_item_factors(key, part):
    key_base = jax.random.fold_in(jax.random.fold_in(key, 11), 0)
    key_column = jax.random.fold_in(jax.random.fold_in(key, 11), 3)
    position = jnp.arange(ITEMS, dtype=jnp.float32) / ITEMS
    row_scale = (1.0 + 2.0 * position) / math.sqrt(RANK)
    column_scale = jnp.exp(jax.random.uniform(key_column, (1, RANK), jnp.float32, math.log(0.3), 0.0))
    values = jax.random.normal(key_base, (ITEMS, RANK), jnp.float32)
    return (row_scale[:, None] * values * column_scale).astype(jnp.bfloat16)


def draw_confidence(key, part):
    key_mask, key_forced, key_value = jax.random.split(jax.random.fold_in(key, 23), 3)
    shape = (ALL_TILES, BLOCK, BLOCK)
    chance = jax.random.uniform(key_mask, shape, jnp.float32)
    forced = jax.random.randint(key_forced, (ALL_TILES, BLOCK, 1), 0, BLOCK)
    columns = jnp.arange(BLOCK, dtype=jnp.int32)[None, None, :]
    observed = jnp.logical_or(chance < 0.5, columns == forced)
    values = jnp.exp(jax.random.uniform(key_value, shape, jnp.float32, math.log(4.0), math.log(160.0)))
    return jnp.where(observed, values, 0.0).astype(jnp.bfloat16)


def set_ends(array, stream_key, smallest, high):
    longest = array.shape.index(max(array.shape))
    spots = []
    for shift in (0, 1):
        where = [jax.random.randint(jax.random.fold_in(stream_key, axis), (), 0, length) for axis, length in enumerate(array.shape)]
        where[longest] = (where[longest] + shift) % array.shape[longest]
        spots.append(tuple(where))
    return array.at[spots[0]].set(smallest).at[spots[1]].set(high)


def setup_inputs(seed: int = 0) -> dict:
    key_list = jax.random.split(jax.random.key(seed), 6)
    return {
        "item_factors": draw_item_factors(jax.random.fold_in(key_list[5], 71), 0),
        "send_list": set_ends(jax.random.randint(key_list[1], (N_GRP * N_DEV, N_GRP, SENT), 0, PANELS_DEV), jax.random.fold_in(key_list[1], 1), 0, PANELS_DEV - 1).astype(jnp.int32),
        "route_list": set_ends(jax.random.randint(key_list[2], (N_GRP * N_DEV, N_DEV, PICKED), 0, N_GRP * SENT), jax.random.fold_in(key_list[2], 1), 0, (N_GRP * SENT) - 1).astype(jnp.int32),
        "tile_slot": set_ends(jax.random.randint(key_list[3], (N_GRP * N_DEV, TILES), 0, N_DEV * PICKED), jax.random.fold_in(key_list[3], 1), 0, (N_DEV * PICKED) - 1).astype(jnp.int32),
        "confidence": draw_confidence(jax.random.fold_in(key_list[5], 71), 0),
    }


ridge = 0.1


def apply_operator(direction, gram, tile_panels, weights):
    dir_bf = direction.astype(jnp.bfloat16).astype(jnp.float32).reshape(USER_BLOCKS, BLOCK, RANK)
    panels32 = tile_panels.astype(jnp.float32)
    scores = jnp.einsum('ubr,utir->utbi', dir_bf, panels32)
    weighted = (weights.astype(jnp.float32) * scores).astype(jnp.bfloat16).astype(jnp.float32)
    back = jnp.einsum('utbi,utir->ubr', weighted, panels32).reshape(USER_BLOCKS * BLOCK, RANK)
    return jnp.dot(direction, gram, precision=lax.Precision.HIGHEST) + ridge * direction + back


def solve_users(gram, tile_panels, weights):
    observed = (weights > 0).astype(jnp.float32)
    target = ((1.0 + weights.astype(jnp.float32)) * observed).astype(jnp.bfloat16).astype(jnp.float32)
    right_side = jnp.einsum('utbi,utir->ubr', target, tile_panels.astype(jnp.float32)).reshape(USER_BLOCKS * BLOCK, RANK)
    solution = jnp.zeros_like(right_side)
    residual = right_side
    direction = right_side
    norm_now = jnp.sum(residual * residual, axis=1, keepdims=True)
    for step in range(ITERS):
        image = apply_operator(direction, gram, tile_panels, weights)
        alpha = norm_now / jnp.sum(direction * image, axis=1, keepdims=True)
        solution = solution + alpha * direction
        residual = residual - alpha * image
        norm_next = jnp.sum(residual * residual, axis=1, keepdims=True)
        direction = residual + (norm_next / norm_now) * direction
        norm_now = norm_next
    return solution


def reference(item_factors, send_list, route_list, tile_slot, confidence):
    devices = N_GRP * N_DEV
    gram = jnp.dot(item_factors.T, item_factors, preferred_element_type=jnp.float32)
    panels = item_factors.reshape(devices * PANELS_DEV, BLOCK, RANK)
    device_ids = jnp.arange(devices, dtype=jnp.int32)
    group_of = (device_ids // N_DEV)[:, None]
    member_of = (device_ids % N_DEV)[:, None]
    source_dev = (tile_slot // PICKED).astype(jnp.int32)
    picked_at = (tile_slot % PICKED).astype(jnp.int32)
    pool_index = route_list[group_of * N_DEV + source_dev, member_of, picked_at]
    anchor_group = (pool_index // SENT).astype(jnp.int32)
    sent_at = (pool_index % SENT).astype(jnp.int32)
    owner = anchor_group * N_DEV + source_dev
    local_panel = send_list[owner, group_of, sent_at]
    global_panel = (owner * PANELS_DEV + local_panel).astype(jnp.int32)
    weights_all = confidence.reshape(devices, USER_BLOCKS, TILES_PER, BLOCK, BLOCK)

    def one_device(pair):
        panel_ids, weights = pair
        tile_panels = panels[panel_ids].reshape(USER_BLOCKS, TILES_PER, BLOCK, RANK)
        return solve_users(gram, tile_panels, weights)

    solved = lax.map(one_device, (global_panel, weights_all))
    return solved.reshape(USERS, RANK)
```

```python
import functools

import jax
import jax.numpy as jnp
from jax import lax
from jax.experimental import pallas as pl
from jax.experimental.pallas import tpu as pltpu
from jax.sharding import PartitionSpec as P

PANELS_DEV=2; RANK=256; BLOCK=128; UB=4; TP=16; ITERS=8; RIDGE=0.1
F32=jnp.float32; BF=jnp.bfloat16
NT=(((1,),(1,)),((),()))
def dot(a,b): return jnp.dot(a,b,preferred_element_type=F32)

def cg_kernel(CH, PT, slot_ref, gram_ref, conf_ref, slots_ref, out_ref, pan, pant, gh, gl, res, dirn, rr):
    W=UB*TP
    def gather(t,_):
        p=slots_ref[slot_ref[0,t]]
        pan[pl.ds(pl.multiple_of(t*BLOCK,BLOCK),BLOCK),:]=p
        return 0
    lax.fori_loop(0,W,gather,0,unroll=4)
    if PT:
        def tr(q,_):
            p=pan[pl.ds(pl.multiple_of(q*256,256),256),:]
            pant[pl.ds(pl.multiple_of(q*256,256),256),:]=p.T
            return 0
        lax.fori_loop(0,W//2,tr,0)
    g=gram_ref[...]
    h=g.astype(BF); gh[...]=h; gl[...]=(g-h.astype(F32)).astype(BF)
    NC=TP*BLOCK//CH; TC=CH//BLOCK
    def tiles(b,c): return [b*TP+c*TC+j for j in range(TC)]
    def rows(b,c): return slice((b*TP+c*TC)*BLOCK,(b*TP+c*TC+TC)*BLOCK)
    for b in range(UB):
        acc=None
        for c in range(NC):
            w=jnp.concatenate([conf_ref[t] for t in tiles(b,c)],axis=1).astype(F32)
            tgt=jnp.where(w>0,1.0+w,0.0).astype(BF)
            d=dot(tgt,pan[rows(b,c),:])
            acc=d if acc is None else acc+d
        us=slice(b*BLOCK,(b+1)*BLOCK)
        res[us,:]=acc; dirn[us,:]=acc
        out_ref[us,:]=jnp.zeros_like(acc)
        rr[us,:]=jnp.broadcast_to(jnp.sum(acc*acc,axis=1,keepdims=True),(BLOCK,128))
    def it(i,_):
        for b in range(UB):
            us=slice(b*BLOCK,(b+1)*BLOCK)
            v=dirn[us,:]
            vb=v.astype(BF); vl=(v-vb.astype(F32)).astype(BF)
            acc=dot(vb,gh[...])+dot(vb,gl[...])+dot(vl,gh[...])+RIDGE*v
            for c in range(NC):
                if PT:
                    s=jnp.concatenate([dot(vb,pant[(b*TP+c*TC+2*j)*BLOCK:(b*TP+c*TC+2*j+2)*BLOCK,:]) for j in range(TC//2)],axis=1)
                else:
                    s=lax.dot_general(vb,pan[rows(b,c),:],NT,preferred_element_type=F32)
                w=jnp.concatenate([conf_ref[t] for t in tiles(b,c)],axis=1).astype(F32)
                ws=(w*s).astype(BF)
                acc=acc+dot(ws,pan[rows(b,c),:])
            r0=rr[us,0:1]
            alpha=r0/jnp.sum(v*acc,axis=1,keepdims=True)
            out_ref[us,:]=out_ref[us,:]+alpha*v
            r=res[us,:]-alpha*acc
            r1=jnp.sum(r*r,axis=1,keepdims=True)
            res[us,:]=r
            dirn[us,:]=r+(r1/r0)*v
            rr[us,:]=jnp.broadcast_to(r1,(BLOCK,128))
        return 0
    lax.fori_loop(0,ITERS,it,0)

def cg(slot, gram, conf, slots, CH=512, PT=False):
    vm=pl.BlockSpec(memory_space=pltpu.VMEM)
    return pl.pallas_call(functools.partial(cg_kernel,CH,PT),
        out_shape=jax.ShapeDtypeStruct((UB*BLOCK,RANK),F32),
        in_specs=[pl.BlockSpec(memory_space=pltpu.SMEM),vm,vm,vm], out_specs=vm,
        scratch_shapes=[pltpu.VMEM((UB*TP*BLOCK,RANK),BF),pltpu.VMEM((UB*TP*BLOCK,RANK),BF),
          pltpu.VMEM((RANK,RANK),BF),pltpu.VMEM((RANK,RANK),BF),
          pltpu.VMEM((UB*BLOCK,RANK),F32),pltpu.VMEM((UB*BLOCK,RANK),F32),pltpu.VMEM((UB*BLOCK,128),F32)],
        name="cg", compiler_params=pltpu.CompilerParams(vmem_limit_bytes=48<<20))(slot,gram,conf,slots)


MESH = pl.DeviceIdType.MESH
NG, NX, NZ = 8, 4, 8
ND = NX * NZ
HALF1 = ((4, 0), (3, 0), (5, 0), (2, 0), (6, 0))


def comm_kernel(order, split, send_ref, route_ref, items_ref, slots_ref, gram_ref,
                pool, out1, out2, part, g1, g2, g3, s2, s3, s4,
                ss1, rs1, ss2, rs2, gs1, gr1, gs2, gr2, gs3, gr3, gs4, gr4, gs5, gr5):
    g = lax.axis_index("grp")
    d = lax.axis_index("dev")
    z, x = d // NX, lax.rem(d, NX)
    grp_peers = [lax.rem(g + k, NG) for k in range(1, NG)]
    x_peers = [lax.rem(x + k, NX) for k in range(1, NX)]
    z_peers = [lax.rem(z + k, NZ) for k in range(1, NZ)]

    barrier = pltpu.get_barrier_semaphore()
    for p in grp_peers:
        pl.semaphore_signal(barrier, inc=1, device_id={"grp": p}, device_id_type=MESH)
    for k in range(1, ND):
        pl.semaphore_signal(barrier, inc=1, device_id={"dev": lax.rem(d + k, ND)}, device_id_type=MESH)

    def send(src, dst, ss, rs, where):
        c = pltpu.make_async_remote_copy(
            src_ref=src, dst_ref=dst, send_sem=ss, recv_sem=rs, device_id=where, device_id_type=MESH)
        c.start()
        return c

    def arrived(ref, ss, rs, where):
        pltpu.make_async_remote_copy(
            src_ref=ref, dst_ref=ref, send_sem=ss, recv_sem=rs, device_id=where, device_id_type=MESH).wait_recv()

    flat = items_ref[...].reshape(PANELS_DEV * BLOCK, RANK)
    part[...] = lax.dot_general(flat, flat, (((0,), (0,)), ((), ())), preferred_element_type=F32)
    for j in range(NG):
        out1[j] = items_ref[send_ref[0, j, 0]]
    pool[g] = out1[g]
    g1[g] = part[pl.ds(pl.multiple_of(g * 32, 32), 32), :]
    pl.semaphore_wait(barrier, NG - 1 + ND - 1)

    sent = []
    for p in grp_peers:
        sent.append(send(part.at[pl.ds(pl.multiple_of(p * 32, 32), 32), :], g1.at[g], gs1.at[p], gr1.at[g], {"grp": p}))
    for p in grp_peers:
        sent.append(send(out1.at[p], pool.at[g], ss1.at[p], rs1.at[g], {"grp": p}))
    for p in grp_peers:
        arrived(g1.at[p], gs1.at[p], gr1.at[p], {"grp": p})
    total = g1[0]
    for j in range(1, NG):
        total = total + g1[j]
    s2[...] = total.reshape(NX, 8, RANK)
    g2[x] = s2[x]
    for p in x_peers:
        sent.append(send(s2.at[p], g2.at[x], gs2.at[p], gr2.at[x], {"dev": z * NX + p}))
    for p in x_peers:
        arrived(g2.at[p], gs2.at[p], gr2.at[p], {"dev": z * NX + p})
    s3[...] = (g2[0] + g2[1]) + (g2[2] + g2[3])
    g3[z] = s3[...]
    for p in z_peers:
        sent.append(send(s3, g3.at[z], gs3.at[p], gr3.at[z], {"dev": p * NX + x}))

    for p in grp_peers:
        arrived(pool.at[p], ss1.at[p], rs1.at[p], {"grp": p})

    dests = [(lax.rem(z + dz, NZ) * NX + lax.rem(x + dx, NX)) for dz, dx in order]

    def fill(e):
        out2[e] = pool[route_ref[0, e, 0]]

    def ship(e):
        sent.append(send(out2.at[e], slots_ref.at[d], ss2.at[e], rs2.at[d], {"dev": e}))

    fill(dests[0])
    fill(dests[1])
    for i in range(len(dests)):
        if i + 2 < len(dests):
            fill(dests[i + 2])
        ship(dests[i])
        if i == split:
            for p in z_peers:
                arrived(g3.at[p], gs3.at[p], gr3.at[p], {"dev": p * NX + x})
            tot = g3[0]
            for j in range(1, NZ):
                tot = tot + g3[j]
            s4[x] = tot
            for p in x_peers:
                sent.append(send(s4.at[x], s4.at[x], gs4.at[p], gr4.at[x], {"dev": z * NX + p}))
    slots_ref[d] = pool[route_ref[0, d, 0]]
    for p in x_peers:
        arrived(s4.at[p], gs4.at[p], gr4.at[p], {"dev": z * NX + p})
    gram_ref[g] = s4[...]
    for p in grp_peers:
        sent.append(send(s4, gram_ref.at[g], gs5.at[p], gr5.at[g], {"grp": p}))
    for p in grp_peers:
        arrived(gram_ref.at[p], gs5.at[p], gr5.at[p], {"grp": p})
    for e in dests:
        arrived(slots_ref.at[e], ss2.at[e], rs2.at[e], {"dev": e})
    for c in sent:
        c.wait_send()


ORDER = tuple((dz, dx) for dz in (4, 3, 5, 2, 6, 1, 7, 0) for dx in range(NX) if (dz, dx) != (0, 0))


def comm(send_list, route_list, items, order=ORDER, split=15):
    vm = pl.BlockSpec(memory_space=pltpu.VMEM)
    sm = pl.BlockSpec(memory_space=pltpu.SMEM)
    dma = pltpu.SemaphoreType.DMA
    slots, gram = pl.pallas_call(
        functools.partial(comm_kernel, order, split),
        out_shape=(jax.ShapeDtypeStruct((ND, BLOCK, RANK), BF), jax.ShapeDtypeStruct((NG, NX, 8, RANK), F32)),
        in_specs=[sm, sm, vm],
        out_specs=(vm, vm),
        scratch_shapes=[
            pltpu.VMEM((NG, BLOCK, RANK), BF),
            pltpu.VMEM((NG, BLOCK, RANK), BF),
            pltpu.VMEM((ND, BLOCK, RANK), BF),
            pltpu.VMEM((RANK, RANK), F32),
            pltpu.VMEM((NG, 32, RANK), F32),
            pltpu.VMEM((NX, 8, RANK), F32),
            pltpu.VMEM((NZ, 8, RANK), F32),
            pltpu.VMEM((NX, 8, RANK), F32),
            pltpu.VMEM((8, RANK), F32),
            pltpu.VMEM((NX, 8, RANK), F32),
            dma((NG,)), dma((NG,)), dma((ND,)), dma((ND,)),
            dma((NG,)), dma((NG,)), dma((NX,)), dma((NX,)), dma((NZ,)), dma((NZ,)),
            dma((NX,)), dma((NX,)), dma((NG,)), dma((NG,)),
        ],
        name="exchange",
        compiler_params=pltpu.CompilerParams(collective_id=0, has_side_effects=True, vmem_limit_bytes=32 << 20),
    )(send_list, route_list, items)
    return slots, gram.reshape(RANK, RANK)


def shards(item_factors, send_list, route_list, tile_slot, confidence):
    own_panels = item_factors.reshape(-1, BLOCK, RANK)
    slots, gram = comm(send_list, route_list, own_panels)
    return cg(tile_slot, gram, confidence, slots, CH=1024, PT=True)


def solution(mesh):
    placed = (
        P(("grp", "dev"), None),
        P(("grp", "dev"), None, None),
        P(("grp", "dev"), None, None),
        P(("grp", "dev"), None),
        P(("grp", "dev"), None, None),
    )
    return jax.shard_map(
        shards, mesh=mesh, in_specs=placed, out_specs=P(("grp", "dev"), None), check_vma=False
    )
```

```python
import functools

import jax
import jax.numpy as jnp
from jax import lax
from jax.experimental import pallas as pl
from jax.experimental.pallas import tpu as pltpu
from jax.sharding import PartitionSpec as P

PANELS_DEV = 2
RANK = 256
BLOCK = 128
UB = 4
TP = 16
ITERS = 8
RIDGE = 0.1
NG, NY, NC, NX, NZ = 8, 4, 2, 4, 8
ND = NX * NZ
SEND_AT, ROUTE_AT, SLOT_AT = 0, 8, 40
F32 = jnp.float32
BF = jnp.bfloat16
MESH = pl.DeviceIdType.MESH
FAR = (3, 5, 4)
NEAR = tuple((dz, dx) for dz in (2, 6, 1, 7, 0) for dx in (2, 1, 3, 0) if (dz, dx) != (0, 0))
FIRST = 10
CHUNK = 1024


def dot(a, b):
    return jnp.dot(a, b, preferred_element_type=F32)


def half(ref, i):
    return ref.at[pl.ds(pl.multiple_of(i * 128, 128), 128), :]


def solve(meta, slots, gram, conf, out, pan, pant, gh, gl, res, dirn, rr):
    tiles = UB * TP

    def gather(t, carry):
        pan[pl.ds(pl.multiple_of(t * BLOCK, BLOCK), BLOCK), :] = slots[meta[0, SLOT_AT + t]]
        return carry

    lax.fori_loop(0, tiles, gather, 0, unroll=4)

    def turn(q, carry):
        rows = pl.ds(pl.multiple_of(q * 256, 256), 256)
        pant[rows, :] = pan[rows, :].T
        return carry

    lax.fori_loop(0, tiles // 2, turn, 0)
    g = gram[...].reshape(RANK, RANK)
    high = g.astype(BF)
    gh[...] = high
    gl[...] = (g - high.astype(F32)).astype(BF)
    per = CHUNK // BLOCK
    chunks = TP // per

    def confs(b, c):
        return jnp.concatenate([conf[b * TP + c * per + j] for j in range(per)], axis=1).astype(F32)

    def rows(b, c):
        return slice((b * TP + c * per) * BLOCK, (b * TP + c * per + per) * BLOCK)

    for b in range(UB):
        acc = None
        for c in range(chunks):
            w = confs(b, c)
            d = dot(jnp.where(w > 0, 1.0 + w, 0.0).astype(BF), pan[rows(b, c), :])
            acc = d if acc is None else acc + d
        us = slice(b * BLOCK, (b + 1) * BLOCK)
        res[us, :] = acc
        dirn[us, :] = acc
        out[us, :] = jnp.zeros_like(acc)
        rr[us, :] = jnp.broadcast_to(jnp.sum(acc * acc, axis=1, keepdims=True), (BLOCK, 128))

    def step(i, carry):
        for b in range(UB):
            us = slice(b * BLOCK, (b + 1) * BLOCK)
            v = dirn[us, :]
            vb = v.astype(BF)
            vl = (v - vb.astype(F32)).astype(BF)
            acc = dot(vb, gh[...]) + dot(vb, gl[...]) + dot(vl, gh[...]) + RIDGE * v
            for c in range(chunks):
                first = (b * TP + c * per) * BLOCK
                s = jnp.concatenate(
                    [dot(vb, pant[first + 256 * j : first + 256 * j + 256, :]) for j in range(per // 2)], axis=1
                )
                acc = acc + dot((confs(b, c) * s).astype(BF), pan[rows(b, c), :])
            old = rr[us, 0:1]
            alpha = old / jnp.sum(v * acc, axis=1, keepdims=True)
            out[us, :] = out[us, :] + alpha * v
            r = res[us, :] - alpha * acc
            new = jnp.sum(r * r, axis=1, keepdims=True)
            res[us, :] = r
            dirn[us, :] = r + (new / old) * v
            rr[us, :] = jnp.broadcast_to(new, (BLOCK, 128))
        return carry

    lax.fori_loop(0, ITERS, step, 0)


def exchange(meta_v, meta, items, slots, gram, raw, metas_v, metas, pools, out1, out2, out3, part,
             gc, sc, gy, s2, g2, s3, g3, s4, local, sm, rm, sr, rr, sp, rp, sn, rs, sx,
             cs, cr, ys, yr, xs, xr, zs, zr, as_, ar, bs, br, es, er, before_wait):
    g = lax.axis_index("grp")
    d = lax.axis_index("dev")
    z, x = d // NX, lax.rem(d, NX)
    y, c = g // NC, lax.rem(g, NC)
    grp_peers = [lax.rem(g + k, NG) for k in (1, 3, 5, 7, 2, 6, 4)]
    x_peers = [lax.rem(x + k, NX) for k in range(1, NX)]
    y_peers = [lax.rem(y + k, NY) for k in range(1, NY)]
    z_peers = [lax.rem(z + k, NZ) for k in range(1, NZ)]

    def at_z(k):
        return {"dev": lax.rem(z + k, NZ) * NX + x}

    def at_x(p):
        return {"dev": z * NX + p}

    def at_y(p):
        return {"grp": p * NC + c}

    other = {"grp": y * NC + 1 - c}

    barrier = pltpu.get_barrier_semaphore()
    near = [lax.rem(z + dz, NZ) * NX + lax.rem(x + dx, NX) for dz, dx in NEAR]
    for p in grp_peers:
        pl.semaphore_signal(barrier, inc=1, device_id={"grp": p}, device_id_type=MESH)
    for e in near:
        pl.semaphore_signal(barrier, inc=1, device_id={"dev": e}, device_id_type=MESH)
    for o in FAR:
        pl.semaphore_signal(barrier, inc=1, device_id=at_z(o), device_id_type=MESH)

    started = []

    def send(src, dst, ss, rs_, where):
        copy = pltpu.make_async_remote_copy(
            src_ref=src, dst_ref=dst, send_sem=ss, recv_sem=rs_, device_id=where, device_id_type=MESH
        )
        copy.start()
        started.append(copy)

    def arrived(ref, ss, rs_):
        pltpu.make_async_remote_copy(
            src_ref=ref, dst_ref=ref, send_sem=ss, recv_sem=rs_, device_id=other, device_id_type=MESH
        ).wait_recv()

    before_wait()
    flat = items[...].reshape(PANELS_DEV * BLOCK, RANK)
    part[...] = lax.dot_general(flat, flat, (((0,), (0,)), ((), ())), preferred_element_type=F32)
    for j in range(NG):
        out1[3, j] = items[meta[0, SEND_AT + j]]
    pools[3][g] = out1[3, g]
    pl.semaphore_wait(barrier, len(grp_peers) + len(near) + len(FAR))

    for i, o in enumerate(FAR):
        send(meta_v, metas_v.at[i], sm.at[i], rm.at[i], at_z(NZ - o))
    for i in range(2):
        send(items, raw[i], sr.at[i], rr.at[i], at_z(NZ - FAR[i]))
    for p in grp_peers:
        send(out1.at[3, p], pools[3].at[g], sp.at[3, p], rp.at[3, g], {"grp": p})
    send(half(part, 1 - c), gc, cs.at[0], cr.at[0], other)
    arrived(gc, cs.at[0], cr.at[0])
    sc[...] = (half(part, c)[...] + gc[...]).reshape(NY, 32, RANK)
    gy[y] = sc[y]
    for p in y_peers:
        send(sc.at[p], gy.at[y], ys.at[p], yr.at[y], at_y(p))

    def pool_ready(i):
        for p in grp_peers:
            arrived(pools[i].at[p], sp.at[i, p], rp.at[i, p])

    def fill(n):
        if n < len(near):
            out2[n] = pools[3][meta[0, ROUTE_AT + near[n]]]

    def ship(n):
        send(out2.at[n], slots.at[d], sn.at[n], rs.at[d], {"dev": near[n]})

    pool_ready(3)
    fill(0)
    fill(1)
    for n in range(FIRST):
        fill(n + 2)
        ship(n)
    for p in y_peers:
        arrived(gy.at[p], ys.at[p], yr.at[p])
    s2[...] = ((gy[0] + gy[1]) + (gy[2] + gy[3])).reshape(NX, 8, RANK)
    g2[x] = s2[x]
    for p in x_peers:
        send(s2.at[p], g2.at[x], xs.at[p], xr.at[x], at_x(p))

    def proxy(i):
        for j in range(NG):
            out1[i, j] = raw[i][metas[i, 0, SEND_AT + j]]
        pools[i][g] = out1[i, g]
        for p in grp_peers:
            send(out1.at[i, p], pools[i].at[g], sp.at[i, p], rp.at[i, g], {"grp": p})

    for i in range(3):
        arrived(metas_v.at[i], sm.at[i], rm.at[i])
        pltpu.make_async_copy(metas_v.at[i], metas.at[i], local.at[i]).start()
    for i in range(3):
        pltpu.make_async_copy(metas_v.at[i], metas.at[i], local.at[i]).wait()
    arrived(raw[0], sr.at[0], rr.at[0])
    send(raw[0].at[1], raw[2].at[1], sr.at[3], rr.at[3], at_z(NZ - 1))
    arrived(raw[1], sr.at[1], rr.at[1])
    send(raw[1].at[0], raw[2].at[0], sr.at[2], rr.at[2], at_z(1))
    proxy(0)
    proxy(1)

    for p in x_peers:
        arrived(g2.at[p], xs.at[p], xr.at[p])
    s3[...] = (g2[0] + g2[1]) + (g2[2] + g2[3])
    g3[z] = s3[...]
    for k, p in enumerate(z_peers):
        send(s3, g3.at[z], zs.at[p], zr.at[z], at_z(k + 1))

    for n in range(FIRST, len(near)):
        fill(n + 2)
        ship(n)

    arrived(raw[2].at[0], sr.at[2], rr.at[2])
    arrived(raw[2].at[1], sr.at[3], rr.at[3])
    proxy(2)

    for p in z_peers:
        arrived(g3.at[p], zs.at[p], zr.at[p])
    total = ((g3[0] + g3[1]) + (g3[2] + g3[3])) + ((g3[4] + g3[5]) + (g3[6] + g3[7]))
    s4[x] = total
    for p in x_peers:
        send(s4.at[x], s4.at[x], as_.at[p], ar.at[x], at_x(p))

    def relay(i):
        slot = lax.rem(z + FAR[i], NZ) * NX + x
        pool_ready(i)
        for k, p in enumerate(x_peers):
            out3[i, k] = pools[i][metas[i, 0, ROUTE_AT + z * NX + p]]
        for k, p in enumerate(x_peers):
            send(out3.at[i, k], slots.at[slot], sx.at[i, k], rs.at[slot], at_x(p))
        slots[slot] = pools[i][metas[i, 0, ROUTE_AT + d]]

    slots[d] = pools[3][meta[0, ROUTE_AT + d]]
    relay(0)
    relay(1)
    for p in x_peers:
        arrived(s4.at[p], as_.at[p], ar.at[p])
    gram[c, y] = s4[...]
    for p in y_peers:
        send(s4, gram.at[c, y], bs.at[p], br.at[y], at_y(p))
    relay(2)
    for p in y_peers:
        arrived(gram.at[c, p], bs.at[p], br.at[p])
    send(gram.at[c], gram.at[c], es.at[0], er.at[0], other)

    for n, e in enumerate(near):
        arrived(slots.at[e], sn.at[n], rs.at[e])
    for i, o in enumerate(FAR):
        for k, p in enumerate(x_peers):
            slot = lax.rem(z + o, NZ) * NX + p
            arrived(slots.at[slot], sx.at[i, k], rs.at[slot])
    arrived(gram.at[1 - c], es.at[0], er.at[0])
    for copy in started:
        copy.wait_send()


def kernel(meta_h, items_h, conf_h, out, meta_v, meta, items, conf, slots, gram, raw0, raw1, raw2, metas_v, metas,
           pool0, pool1, pool2, pool3, out1, out2, out3, part, gc, sc, gy, s2, g2, s3, g3, s4, pan, pant, gh, gl, res, dirn, rr, *sems):
    ins, sems = sems[0], sems[1:]
    loads = [
        pltpu.make_async_copy(meta_h, meta, ins.at[0]),
        pltpu.make_async_copy(meta_h, meta_v, ins.at[1]),
        pltpu.make_async_copy(items_h, items, ins.at[2]),
        pltpu.make_async_copy(conf_h, conf, ins.at[3]),
    ]
    for copy in loads:
        copy.start()

    def ready():
        for copy in loads[:3]:
            copy.wait()

    exchange(meta_v, meta, items, slots, gram, (raw0, raw1, raw2), metas_v, metas,
             (pool0, pool1, pool2, pool3), out1, out2, out3, part,
             gc, sc, gy, s2, g2, s3, g3, s4, *sems, ready)
    loads[3].wait()
    solve(meta, slots, gram, conf, out, pan, pant, gh, gl, res, dirn, rr)


def half_sweep(meta, items, conf):
    dma = pltpu.SemaphoreType.DMA
    hbm = pl.BlockSpec(memory_space=pl.ANY)
    panel = (BLOCK, RANK)
    users = UB * BLOCK
    return pl.pallas_call(
        kernel,
        out_shape=jax.ShapeDtypeStruct((users, RANK), F32),
        in_specs=[hbm, hbm, hbm],
        out_specs=pl.BlockSpec(memory_space=pltpu.VMEM),
        scratch_shapes=[
            pltpu.VMEM((1, 128), jnp.int32), pltpu.SMEM((1, 128), jnp.int32),
            pltpu.VMEM((PANELS_DEV, *panel), BF), pltpu.VMEM((UB * TP, BLOCK, BLOCK), BF),
            pltpu.VMEM((ND, *panel), BF), pltpu.VMEM((NC, NY, NX, 8, RANK), F32),
            pltpu.VMEM((PANELS_DEV, *panel), BF), pltpu.VMEM((PANELS_DEV, *panel), BF),
            pltpu.VMEM((PANELS_DEV, *panel), BF),
            pltpu.VMEM((3, 1, 128), jnp.int32), pltpu.SMEM((3, 1, 128), jnp.int32),
            pltpu.VMEM((NG, *panel), BF), pltpu.VMEM((NG, *panel), BF), pltpu.VMEM((NG, *panel), BF),
            pltpu.VMEM((NG, *panel), BF), pltpu.VMEM((4, NG, *panel), BF),
            pltpu.VMEM((len(NEAR), *panel), BF), pltpu.VMEM((3, NX - 1, *panel), BF),
            pltpu.VMEM((RANK, RANK), F32), pltpu.VMEM((128, RANK), F32),
            pltpu.VMEM((NY, 32, RANK), F32), pltpu.VMEM((NY, 32, RANK), F32),
            pltpu.VMEM((NX, 8, RANK), F32), pltpu.VMEM((NX, 8, RANK), F32),
            pltpu.VMEM((8, RANK), F32), pltpu.VMEM((NZ, 8, RANK), F32), pltpu.VMEM((NX, 8, RANK), F32),
            pltpu.VMEM((UB * TP * BLOCK, RANK), BF), pltpu.VMEM((UB * TP * BLOCK, RANK), BF),
            pltpu.VMEM((RANK, RANK), BF), pltpu.VMEM((RANK, RANK), BF),
            pltpu.VMEM((users, RANK), F32), pltpu.VMEM((users, RANK), F32), pltpu.VMEM((users, 128), F32),
            dma((4,)),
            dma((3,)), dma((3,)), dma((3,)),
            dma((4,)), dma((4,)),
            dma((4, NG)), dma((4, NG)),
            dma((len(NEAR),)), dma((ND,)), dma((3, NX - 1)),
            dma((1,)), dma((1,)), dma((NY,)), dma((NY,)), dma((NX,)), dma((NX,)), dma((NZ,)), dma((NZ,)),
            dma((NX,)), dma((NX,)), dma((NY,)), dma((NY,)), dma((1,)), dma((1,)),
        ],
        name="half_sweep",
        compiler_params=pltpu.CompilerParams(collective_id=0, has_side_effects=True, vmem_limit_bytes=60 * 1024 * 1024),
    )(meta, items, conf)


def shards(item_factors, send_list, route_list, tile_slot, confidence):
    meta = jnp.concatenate(
        [send_list.reshape(1, -1), route_list.reshape(1, -1), tile_slot, jnp.zeros((1, 24), jnp.int32)], axis=1
    )
    return half_sweep(meta, item_factors.reshape(-1, BLOCK, RANK), confidence)


def solution(mesh):
    placed = (
        P(("grp", "dev"), None),
        P(("grp", "dev"), None, None),
        P(("grp", "dev"), None, None),
        P(("grp", "dev"), None),
        P(("grp", "dev"), None, None),
    )
    return jax.shard_map(
        shards, mesh=mesh, in_specs=placed, out_specs=P(("grp", "dev"), None), check_vma=False
    )
```

```python
import functools

import jax
import jax.numpy as jnp
from jax import lax
from jax.experimental import pallas as pl
from jax.experimental.pallas import tpu as pltpu
from jax.sharding import PartitionSpec as P

PANELS_DEV = 2
RANK = 256
BLOCK = 128
UB = 4
TP = 16
ITERS = 8
RIDGE = 0.1
NG, NY, NC, NX, NZ = 8, 4, 2, 4, 8
ND = NX * NZ
F32 = jnp.float32
BF = jnp.bfloat16
MESH = pl.DeviceIdType.MESH
FAR = (3, 5, 4)
NEAR = tuple((dz, dx) for dz in (2, 6, 1, 7, 0) for dx in (2, 1, 3, 0) if (dz, dx) != (0, 0))
FIRST = 0
CHUNK = 1024


def dot(a, b):
    return jnp.dot(a, b, preferred_element_type=F32)


def half(ref, i):
    return ref.at[pl.ds(pl.multiple_of(i * 128, 128), 128), :]


def solve(meta, slots, gram, conf, out, pan, pant, gh, gl, res, dirn, rr):
    tiles = UB * TP

    def gather(t, carry):
        pan[pl.ds(pl.multiple_of(t * BLOCK, BLOCK), BLOCK), :] = slots[meta[0, t]]
        return carry

    lax.fori_loop(0, tiles, gather, 0, unroll=4)

    def turn(q, carry):
        rows = pl.ds(pl.multiple_of(q * 256, 256), 256)
        pant[rows, :] = pan[rows, :].T
        return carry

    lax.fori_loop(0, tiles // 2, turn, 0)
    g = gram[...].reshape(RANK, RANK)
    high = g.astype(BF)
    gh[...] = high
    gl[...] = (g - high.astype(F32)).astype(BF)
    per = CHUNK // BLOCK
    chunks = TP // per

    def confs(b, c):
        return jnp.concatenate([conf[b * TP + c * per + j] for j in range(per)], axis=1).astype(F32)

    def rows(b, c):
        return slice((b * TP + c * per) * BLOCK, (b * TP + c * per + per) * BLOCK)

    for b in range(UB):
        acc = None
        for c in range(chunks):
            w = confs(b, c)
            d = dot(jnp.where(w > 0, 1.0 + w, 0.0).astype(BF), pan[rows(b, c), :])
            acc = d if acc is None else acc + d
        us = slice(b * BLOCK, (b + 1) * BLOCK)
        res[us, :] = acc
        dirn[us, :] = acc
        out[us, :] = jnp.zeros_like(acc)
        rr[us, :] = jnp.broadcast_to(jnp.sum(acc * acc, axis=1, keepdims=True), (BLOCK, 128))

    def step(i, carry):
        for b in range(UB):
            us = slice(b * BLOCK, (b + 1) * BLOCK)
            v = dirn[us, :]
            vb = v.astype(BF)
            vl = (v - vb.astype(F32)).astype(BF)
            acc = dot(vb, gh[...]) + dot(vb, gl[...]) + dot(vl, gh[...]) + RIDGE * v
            for c in range(chunks):
                first = (b * TP + c * per) * BLOCK
                s = jnp.concatenate(
                    [dot(vb, pant[first + 256 * j : first + 256 * j + 256, :]) for j in range(per // 2)], axis=1
                )
                acc = acc + dot((confs(b, c) * s).astype(BF), pan[rows(b, c), :])
            old = rr[us, 0:1]
            alpha = old / jnp.sum(v * acc, axis=1, keepdims=True)
            out[us, :] = out[us, :] + alpha * v
            r = res[us, :] - alpha * acc
            new = jnp.sum(r * r, axis=1, keepdims=True)
            res[us, :] = r
            dirn[us, :] = r + (new / old) * v
            rr[us, :] = jnp.broadcast_to(new, (BLOCK, 128))
        return carry

    lax.fori_loop(0, ITERS, step, 0)


def exchange(send_v, route_v, send_s, route_s, items, slots, gram, raw, sends_v, routes_v, sends_s, routes_s, pools, out1, out2, out3, part,
             gc, sc, gy, s2, g2, s3, g3, s4, local, sm, rm, sr, rr, sp, rp, sn, rs, sx,
             cs, cr, ys, yr, xs, xr, zs, zr, as_, ar, bs, br, es, er, before_wait):
    g = lax.axis_index("grp")
    d = lax.axis_index("dev")
    z, x = d // NX, lax.rem(d, NX)
    y, c = g // NC, lax.rem(g, NC)
    grp_peers = [lax.rem(g + k, NG) for k in (1, 3, 5, 7, 2, 6, 4)]
    x_peers = [lax.rem(x + k, NX) for k in range(1, NX)]
    y_peers = [lax.rem(y + k, NY) for k in range(1, NY)]
    z_peers = [lax.rem(z + k, NZ) for k in range(1, NZ)]

    def at_z(k):
        return {"dev": lax.rem(z + k, NZ) * NX + x}

    def at_x(p):
        return {"dev": z * NX + p}

    def at_y(p):
        return {"grp": p * NC + c}

    other = {"grp": y * NC + 1 - c}

    barrier = pltpu.get_barrier_semaphore()
    near = [lax.rem(z + dz, NZ) * NX + lax.rem(x + dx, NX) for dz, dx in NEAR]
    for p in grp_peers:
        pl.semaphore_signal(barrier, inc=1, device_id={"grp": p}, device_id_type=MESH)
    for e in near:
        pl.semaphore_signal(barrier, inc=1, device_id={"dev": e}, device_id_type=MESH)
    for o in FAR:
        pl.semaphore_signal(barrier, inc=1, device_id=at_z(o), device_id_type=MESH)

    started = []

    def send(src, dst, ss, rs_, where):
        copy = pltpu.make_async_remote_copy(
            src_ref=src, dst_ref=dst, send_sem=ss, recv_sem=rs_, device_id=where, device_id_type=MESH
        )
        copy.start()
        started.append(copy)

    def arrived(ref, ss, rs_):
        pltpu.make_async_remote_copy(
            src_ref=ref, dst_ref=ref, send_sem=ss, recv_sem=rs_, device_id=other, device_id_type=MESH
        ).wait_recv()

    before_wait()
    flat = items[...].reshape(PANELS_DEV * BLOCK, RANK)
    part[...] = lax.dot_general(flat, flat, (((0,), (0,)), ((), ())), preferred_element_type=F32)
    for j in range(NG):
        out1[3, j] = items[send_s[0, j]]
    pools[3][g] = out1[3, g]
    pl.semaphore_wait(barrier, len(grp_peers) + len(near) + len(FAR))

    for i, o in enumerate(FAR):
        send(send_v, sends_v.at[i], sm.at[0, i], rm.at[0, i], at_z(NZ - o))
        send(route_v, routes_v.at[i], sm.at[1, i], rm.at[1, i], at_z(NZ - o))
    for i in range(2):
        send(items, raw[i], sr.at[i], rr.at[i], at_z(NZ - FAR[i]))
    for p in grp_peers:
        send(out1.at[3, p], pools[3].at[g], sp.at[3, p], rp.at[3, g], {"grp": p})
    send(half(part, 1 - c), gc, cs.at[0], cr.at[0], other)
    arrived(gc, cs.at[0], cr.at[0])
    sc[...] = (half(part, c)[...] + gc[...]).reshape(NY, 32, RANK)
    gy[y] = sc[y]
    for p in y_peers:
        send(sc.at[p], gy.at[y], ys.at[p], yr.at[y], at_y(p))

    def pool_ready(i):
        for p in grp_peers:
            arrived(pools[i].at[p], sp.at[i, p], rp.at[i, p])

    def fill(n):
        if n < len(near):
            out2[n] = pools[3][route_s[0, near[n]]]

    def ship(n):
        send(out2.at[n], slots.at[d], sn.at[n], rs.at[d], {"dev": near[n]})

    pool_ready(3)
    fill(0)
    fill(1)
    for n in range(FIRST):
        fill(n + 2)
        ship(n)
    for p in y_peers:
        arrived(gy.at[p], ys.at[p], yr.at[p])
    s2[...] = ((gy[0] + gy[1]) + (gy[2] + gy[3])).reshape(NX, 8, RANK)
    g2[x] = s2[x]
    for p in x_peers:
        send(s2.at[p], g2.at[x], xs.at[p], xr.at[x], at_x(p))

    def proxy(i):
        for j in range(NG):
            out1[i, j] = raw[i][sends_s[i, 0, j]]
        pools[i][g] = out1[i, g]
        for p in grp_peers:
            send(out1.at[i, p], pools[i].at[g], sp.at[i, p], rp.at[i, g], {"grp": p})

    for i in range(3):
        arrived(sends_v.at[i], sm.at[0, i], rm.at[0, i])
        pltpu.make_async_copy(sends_v.at[i], sends_s.at[i], local.at[0, i]).start()
        arrived(routes_v.at[i], sm.at[1, i], rm.at[1, i])
        pltpu.make_async_copy(routes_v.at[i], routes_s.at[i], local.at[1, i]).start()
    for i in range(3):
        pltpu.make_async_copy(sends_v.at[i], sends_s.at[i], local.at[0, i]).wait()
        pltpu.make_async_copy(routes_v.at[i], routes_s.at[i], local.at[1, i]).wait()
    arrived(raw[0], sr.at[0], rr.at[0])
    send(raw[0].at[1], raw[2].at[1], sr.at[3], rr.at[3], at_z(NZ - 1))
    arrived(raw[1], sr.at[1], rr.at[1])
    send(raw[1].at[0], raw[2].at[0], sr.at[2], rr.at[2], at_z(1))
    proxy(0)
    proxy(1)

    for p in x_peers:
        arrived(g2.at[p], xs.at[p], xr.at[p])
    s3[...] = (g2[0] + g2[1]) + (g2[2] + g2[3])
    g3[z] = s3[...]
    for k, p in enumerate(z_peers):
        send(s3, g3.at[z], zs.at[p], zr.at[z], at_z(k + 1))

    for n in range(FIRST, len(near)):
        fill(n + 2)
        ship(n)

    arrived(raw[2].at[0], sr.at[2], rr.at[2])
    arrived(raw[2].at[1], sr.at[3], rr.at[3])
    proxy(2)

    for p in z_peers:
        arrived(g3.at[p], zs.at[p], zr.at[p])
    total = ((g3[0] + g3[1]) + (g3[2] + g3[3])) + ((g3[4] + g3[5]) + (g3[6] + g3[7]))
    s4[x] = total
    for p in x_peers:
        send(s4.at[x], s4.at[x], as_.at[p], ar.at[x], at_x(p))

    def relay(i):
        slot = lax.rem(z + FAR[i], NZ) * NX + x
        pool_ready(i)
        for k, p in enumerate(x_peers):
            out3[i, k] = pools[i][routes_s[i, 0, z * NX + p]]
        for k, p in enumerate(x_peers):
            send(out3.at[i, k], slots.at[slot], sx.at[i, k], rs.at[slot], at_x(p))
        slots[slot] = pools[i][routes_s[i, 0, d]]

    slots[d] = pools[3][route_s[0, d]]
    relay(0)
    relay(1)
    for p in x_peers:
        arrived(s4.at[p], as_.at[p], ar.at[p])
    gram[c, y] = s4[...]
    for p in y_peers:
        send(s4, gram.at[c, y], bs.at[p], br.at[y], at_y(p))
    relay(2)
    for p in y_peers:
        arrived(gram.at[c, p], bs.at[p], br.at[p])
    send(gram.at[c], gram.at[c], es.at[0], er.at[0], other)

    for n, e in enumerate(near):
        arrived(slots.at[e], sn.at[n], rs.at[e])
    for i, o in enumerate(FAR):
        for k, p in enumerate(x_peers):
            slot = lax.rem(z + o, NZ) * NX + p
            arrived(slots.at[slot], sx.at[i, k], rs.at[slot])
    arrived(gram.at[1 - c], es.at[0], er.at[0])
    for copy in started:
        copy.wait_send()


def kernel(send_h, route_h, slot_h, items_h, conf_h, out, send_v, route_v, send_s, route_s, slot_s, items, conf,
           slots, gram, raw0, raw1, raw2, sends_v, routes_v, sends_s, routes_s, pool0, pool1, pool2, pool3,
           out1, out2, out3, part, gc, sc, gy, s2, g2, s3, g3, s4, pan, pant, gh, gl, res, dirn, rr, *sems):
    ins, sems = sems[0], sems[1:]
    pairs = ((send_h, send_s), (route_h, route_s), (items_h, items), (send_h, send_v), (route_h, route_v),
             (slot_h, slot_s), (conf_h, conf))
    loads = [pltpu.make_async_copy(a, b, ins.at[i]) for i, (a, b) in enumerate(pairs)]
    for copy in loads:
        copy.start()

    def ready():
        for copy in loads[:5]:
            copy.wait()

    exchange(send_v, route_v, send_s, route_s, items, slots, gram, (raw0, raw1, raw2), sends_v, routes_v,
             sends_s, routes_s, (pool0, pool1, pool2, pool3), out1, out2, out3, part,
             gc, sc, gy, s2, g2, s3, g3, s4, *sems, ready)
    loads[5].wait()
    loads[6].wait()
    solve(slot_s, slots, gram, conf, out, pan, pant, gh, gl, res, dirn, rr)


def half_sweep(send_list, route_list, tile_slot, items, conf):
    dma = pltpu.SemaphoreType.DMA
    hbm = pl.BlockSpec(memory_space=pl.ANY)
    panel = (BLOCK, RANK)
    users = UB * BLOCK
    return pl.pallas_call(
        kernel,
        out_shape=jax.ShapeDtypeStruct((users, RANK), F32),
        in_specs=[hbm] * 5,
        out_specs=pl.BlockSpec(memory_space=pltpu.VMEM),
        scratch_shapes=[
            pltpu.VMEM((1, NG), jnp.int32), pltpu.VMEM((1, ND), jnp.int32),
            pltpu.SMEM((1, NG), jnp.int32), pltpu.SMEM((1, ND), jnp.int32), pltpu.SMEM((1, UB * TP), jnp.int32),
            pltpu.VMEM((PANELS_DEV, *panel), BF), pltpu.VMEM((UB * TP, BLOCK, BLOCK), BF),
            pltpu.VMEM((ND, *panel), BF), pltpu.VMEM((NC, NY, NX, 8, RANK), F32),
            pltpu.VMEM((PANELS_DEV, *panel), BF), pltpu.VMEM((PANELS_DEV, *panel), BF),
            pltpu.VMEM((PANELS_DEV, *panel), BF),
            pltpu.VMEM((3, 1, NG), jnp.int32), pltpu.VMEM((3, 1, ND), jnp.int32),
            pltpu.SMEM((3, 1, NG), jnp.int32), pltpu.SMEM((3, 1, ND), jnp.int32),
            pltpu.VMEM((NG, *panel), BF), pltpu.VMEM((NG, *panel), BF), pltpu.VMEM((NG, *panel), BF),
            pltpu.VMEM((NG, *panel), BF), pltpu.VMEM((4, NG, *panel), BF),
            pltpu.VMEM((len(NEAR), *panel), BF), pltpu.VMEM((3, NX - 1, *panel), BF),
            pltpu.VMEM((RANK, RANK), F32), pltpu.VMEM((128, RANK), F32),
            pltpu.VMEM((NY, 32, RANK), F32), pltpu.VMEM((NY, 32, RANK), F32),
            pltpu.VMEM((NX, 8, RANK), F32), pltpu.VMEM((NX, 8, RANK), F32),
            pltpu.VMEM((8, RANK), F32), pltpu.VMEM((NZ, 8, RANK), F32), pltpu.VMEM((NX, 8, RANK), F32),
            pltpu.VMEM((UB * TP * BLOCK, RANK), BF), pltpu.VMEM((UB * TP * BLOCK, RANK), BF),
            pltpu.VMEM((RANK, RANK), BF), pltpu.VMEM((RANK, RANK), BF),
            pltpu.VMEM((users, RANK), F32), pltpu.VMEM((users, RANK), F32), pltpu.VMEM((users, 128), F32),
            dma((7,)),
            dma((2, 3)), dma((2, 3)), dma((2, 3)),
            dma((4,)), dma((4,)),
            dma((4, NG)), dma((4, NG)),
            dma((len(NEAR),)), dma((ND,)), dma((3, NX - 1)),
            dma((1,)), dma((1,)), dma((NY,)), dma((NY,)), dma((NX,)), dma((NX,)), dma((NZ,)), dma((NZ,)),
            dma((NX,)), dma((NX,)), dma((NY,)), dma((NY,)), dma((1,)), dma((1,)),
        ],
        name="half_sweep",
        compiler_params=pltpu.CompilerParams(collective_id=0, has_side_effects=True, vmem_limit_bytes=54000 << 10),
    )(*[pltpu.with_memory_space_constraint(a, pltpu.HBM) for a in (send_list, route_list, tile_slot, items, conf)])


def shards(item_factors, send_list, route_list, tile_slot, confidence):
    return half_sweep(
        send_list.reshape(1, -1), route_list.reshape(1, -1), tile_slot,
        item_factors.reshape(-1, BLOCK, RANK), confidence,
    )


def solution(mesh):
    placed = (
        P(("grp", "dev"), None),
        P(("grp", "dev"), None, None),
        P(("grp", "dev"), None, None),
        P(("grp", "dev"), None),
        P(("grp", "dev"), None, None),
    )
    return jax.shard_map(
        shards, mesh=mesh, in_specs=placed, out_specs=P(("grp", "dev"), None), check_vma=False
    )
```

```python
import functools

import jax
import jax.numpy as jnp
from jax import lax
from jax.experimental import pallas as pl
from jax.experimental.pallas import tpu as pltpu
from jax.sharding import PartitionSpec as P

PANELS_DEV = 2
RANK = 256
BLOCK = 128
UB = 4
TP = 16
ITERS = 8
RIDGE = 0.1
NG, NY, NC, NX, NZ = 8, 4, 2, 4, 8
ND = NX * NZ
F32 = jnp.float32
BF = jnp.bfloat16
MESH = pl.DeviceIdType.MESH
FAR = (3, 5, 4)
NEAR = tuple((dz, dx) for dz in (2, 6, 1, 7, 0) for dx in (2, 1, 3, 0) if (dz, dx) != (0, 0))
NH = 1
HB = BLOCK // NH
PLAN = ("X", "P", "Y", "R", 19, "F", "Z", "L", "A", "M")
CHUNK = 1024
PER = CHUNK // BLOCK
WIDE = True


def dot(a, b):
    return jnp.dot(a, b, preferred_element_type=F32)


def half(ref, i):
    return ref.at[pl.ds(pl.multiple_of(i * 128, 128), 128), :]


def confs(conf, b, c):
    return jnp.concatenate([conf[b * TP + c * PER + j] for j in range(PER)], axis=1).astype(F32)


def chunk(b, c):
    first = (b * TP + c * PER) * BLOCK
    return slice(first, first + CHUNK)


def gather_panels(slot_s, slots, pan, pant):
    def gather(t, carry):
        pan[pl.ds(pl.multiple_of(t * BLOCK, BLOCK), BLOCK), :] = slots[slot_s[0, t]]
        return carry

    lax.fori_loop(0, UB * TP, gather, 0, unroll=4)

    def turn(q, carry):
        rows = pl.ds(pl.multiple_of(q * 256, 256), 256)
        pant[rows, :] = pan[rows, :].T
        return carry

    lax.fori_loop(0, UB * TP // 2, turn, 0)


def right_side(conf, out, pan, res, dirn, rr):
    for b in range(UB):
        acc = None
        for c in range(TP // PER):
            w = confs(conf, b, c)
            d = dot(jnp.where(w > 0, 1.0 + w, 0.0).astype(BF), pan[chunk(b, c), :])
            acc = d if acc is None else acc + d
        us = slice(b * BLOCK, (b + 1) * BLOCK)
        res[us, :] = acc
        dirn[us, :] = acc
        out[us, :] = jnp.zeros_like(acc)
        rr[us, :] = jnp.broadcast_to(jnp.sum(acc * acc, axis=1, keepdims=True), (BLOCK, 128))


def solve(gram, conf, out, pan, pant, gh, gl, res, dirn, rr, gv):
    g = gram[...].reshape(RANK, RANK)
    high = g.astype(BF)
    gh[...] = high
    gl[...] = (g - high.astype(F32)).astype(BF)

    def step(i, carry):
        if WIDE:
            v = dirn[...]
            vb = v.astype(BF)
            vl = (v - vb.astype(F32)).astype(BF)
            gv[...] = dot(vb, gh[...]) + dot(vb, gl[...])
        for b in range(UB):
            us = slice(b * BLOCK, (b + 1) * BLOCK)
            v = dirn[us, :]
            vb = v.astype(BF)
            if WIDE:
                acc = gv[us, :] + RIDGE * v
            else:
                vl = (v - vb.astype(F32)).astype(BF)
                acc = dot(vb, gh[...]) + dot(vb, gl[...]) + dot(vl, gh[...]) + RIDGE * v
            for c in range(TP // PER):
                first = (b * TP + c * PER) * BLOCK
                s = jnp.concatenate(
                    [dot(vb, pant[first + 256 * j : first + 256 * j + 256, :]) for j in range(PER // 2)], axis=1
                )
                acc = acc + dot((confs(conf, b, c) * s).astype(BF), pan[chunk(b, c), :])
            old = rr[us, 0:1]
            alpha = old / jnp.sum(v * acc, axis=1, keepdims=True)
            out[us, :] = out[us, :] + alpha * v
            r = res[us, :] - alpha * acc
            new = jnp.sum(r * r, axis=1, keepdims=True)
            res[us, :] = r
            dirn[us, :] = r + (new / old) * v
            rr[us, :] = jnp.broadcast_to(new, (BLOCK, 128))
        return carry

    lax.fori_loop(0, ITERS, step, 0)


def exchange(send_v, route_v, send_s, route_s, items, slots, gram, raw, sends_v, routes_v, sends_s, routes_s,
             pool, pools, out1, out2, out3, out4, part, gc, sc, gx, s2, g2, s3, g3, s4,
             local, sm, rm, sr, rr, sp, rp, sq, rq, sn, rs, sx,
             cs, cr, ys, yr, xs, xr, zs, zr, as_, ar, bs, br, es, er, before_wait):
    g = lax.axis_index("grp")
    d = lax.axis_index("dev")
    z, x = d // NX, lax.rem(d, NX)
    y, c = g // NC, lax.rem(g, NC)
    grp_peers = [lax.rem(g + k, NG) for k in (1, 3, 5, 7, 2, 6, 4)]
    x_peers = [lax.rem(x + k, NX) for k in range(1, NX)]
    y_peers = [lax.rem(y + k, NY) for k in range(1, NY)]
    z_peers = [lax.rem(z + k, NZ) for k in range(1, NZ)]

    def at_z(k):
        return {"dev": lax.rem(z + k, NZ) * NX + x}

    def at_x(p):
        return {"dev": z * NX + p}

    def at_y(p):
        return {"grp": p * NC + c}

    other = {"grp": y * NC + 1 - c}

    barrier = pltpu.get_barrier_semaphore()
    near = [lax.rem(z + dz, NZ) * NX + lax.rem(x + dx, NX) for dz, dx in NEAR]
    for p in grp_peers:
        pl.semaphore_signal(barrier, inc=1, device_id={"grp": p}, device_id_type=MESH)
    for e in near:
        pl.semaphore_signal(barrier, inc=1, device_id={"dev": e}, device_id_type=MESH)
    for o in FAR:
        pl.semaphore_signal(barrier, inc=1, device_id=at_z(o), device_id_type=MESH)

    started = []

    def send(src, dst, ss, rs_, where):
        copy = pltpu.make_async_remote_copy(
            src_ref=src, dst_ref=dst, send_sem=ss, recv_sem=rs_, device_id=where, device_id_type=MESH
        )
        copy.start()
        started.append(copy)

    def arrived(ref, ss, rs_):
        pltpu.make_async_remote_copy(
            src_ref=ref, dst_ref=ref, send_sem=ss, recv_sem=rs_, device_id=other, device_id_type=MESH
        ).wait_recv()

    before_wait()
    flat = items[...].reshape(PANELS_DEV * BLOCK, RANK)
    part[...] = lax.dot_general(flat, flat, (((0,), (0,)), ((), ())), preferred_element_type=F32)
    for j in range(NG):
        out1[j] = items[send_s[0, j]]
    pool[g] = out1[g]
    pl.semaphore_wait(barrier, len(grp_peers) + len(near) + len(FAR))

    for i, o in enumerate(FAR):
        send(send_v, sends_v.at[i], sm.at[0, i], rm.at[0, i], at_z(NZ - o))
        send(route_v, routes_v.at[i], sm.at[1, i], rm.at[1, i], at_z(NZ - o))
    def rows(h):
        return slice(h * HB, h * HB + HB)

    def send_raw(h):
        for i in range(2):
            send(items.at[:, rows(h), :], raw[i][h], sr.at[h, i], rr.at[h, i], at_z(NZ - FAR[i]))

    send_raw(0)
    for p in grp_peers:
        send(out1.at[p], pool.at[g], sp.at[p], rp.at[g], {"grp": p})
    for h in range(1, NH):
        send_raw(h)
    send(half(part, 1 - c), gc, cs.at[0], cr.at[0], other)
    arrived(gc, cs.at[0], cr.at[0])
    sc[...] = (half(part, c)[...] + gc[...]).reshape(NX, 32, RANK)
    gx[x] = sc[x]
    for p in x_peers:
        send(sc.at[p], gx.at[x], xs.at[p], xr.at[x], at_x(p))

    def fill(n):
        if n < len(near):
            out2[n] = pool[route_s[0, near[n]]]

    def ship(first, last):
        for n in range(first, last):
            fill(n + 2)
            send(out2.at[n], slots.at[d], sn.at[n], rs.at[0, d], {"dev": near[n]})

    def proxy(i, h):
        for j in range(NG):
            out4[i, h, j] = raw[i][h][sends_s[i, 0, j]]
        pools[i][h][g] = out4[i, h, g]
        for p in grp_peers:
            send(out4.at[i, h, p], pools[i][h].at[g], sq.at[i, h, p], rq.at[i, h, g], {"grp": p})

    for i in range(3):
        arrived(sends_v.at[i], sm.at[0, i], rm.at[0, i])
        pltpu.make_async_copy(sends_v.at[i], sends_s.at[i], local.at[0, i]).start()
        arrived(routes_v.at[i], sm.at[1, i], rm.at[1, i])
        pltpu.make_async_copy(routes_v.at[i], routes_s.at[i], local.at[1, i]).start()
    for i in range(3):
        pltpu.make_async_copy(sends_v.at[i], sends_s.at[i], local.at[0, i]).wait()
        pltpu.make_async_copy(routes_v.at[i], routes_s.at[i], local.at[1, i]).wait()

    def raw_in(h):
        arrived(raw[0][h], sr.at[h, 0], rr.at[h, 0])
        send(raw[0][h].at[1], raw[2][h].at[1], sr.at[h, 3], rr.at[h, 3], at_z(NZ - 1))
        arrived(raw[1][h], sr.at[h, 1], rr.at[h, 1])
        send(raw[1][h].at[0], raw[2][h].at[0], sr.at[h, 2], rr.at[h, 2], at_z(1))
        proxy(0, h)
        proxy(1, h)

    def relay(i, h):
        slot = lax.rem(z + FAR[i], NZ) * NX + x
        for p in grp_peers:
            arrived(pools[i][h].at[p], sq.at[i, h, p], rq.at[i, h, p])
        for k, p in enumerate(x_peers):
            out3[i, h, k] = pools[i][h][routes_s[i, 0, z * NX + p]]
        for k, p in enumerate(x_peers):
            send(out3.at[i, h, k], slots.at[slot, rows(h), :], sx.at[i, h, k], rs.at[h, slot], at_x(p))
        slots[slot, rows(h), :] = pools[i][h][routes_s[i, 0, d]]

    def pool_in():
        for p in grp_peers:
            arrived(pool.at[p], sp.at[p], rp.at[p])
        fill(0)
        fill(1)
        slots[d] = pool[route_s[0, d]]

    def gram_x():
        for p in x_peers:
            arrived(gx.at[p], xs.at[p], xr.at[p])
        s2[...] = ((gx[0] + gx[1]) + (gx[2] + gx[3])).reshape(NY, 8, RANK)
        g2[y] = s2[y]
        for p in y_peers:
            send(s2.at[p], g2.at[y], ys.at[p], yr.at[y], at_y(p))

    def gram_y():
        for p in y_peers:
            arrived(g2.at[p], ys.at[p], yr.at[p])
        s3[...] = (g2[0] + g2[1]) + (g2[2] + g2[3])
        g3[z] = s3[...]
        for k, p in enumerate(z_peers):
            send(s3, g3.at[z], zs.at[p], zr.at[z], at_z(k + 1))

    def far_in():
        for h in range(NH):
            arrived(raw[2][h].at[0], sr.at[h, 2], rr.at[h, 2])
            arrived(raw[2][h].at[1], sr.at[h, 3], rr.at[h, 3])
            proxy(2, h)

    def gram_z():
        for p in z_peers:
            arrived(g3.at[p], zs.at[p], zr.at[p])
        s4[x] = ((g3[0] + g3[1]) + (g3[2] + g3[3])) + ((g3[4] + g3[5]) + (g3[6] + g3[7]))
        for p in x_peers:
            send(s4.at[x], s4.at[x], as_.at[p], ar.at[x], at_x(p))

    def gram_back():
        for p in x_peers:
            arrived(s4.at[p], as_.at[p], ar.at[p])
        gram[c, :, y] = s4[...]
        for p in y_peers:
            send(s4, gram.at[c, :, y], bs.at[p], br.at[y], at_y(p))

    def relay_near():
        for h in range(NH):
            relay(0, h)
            relay(1, h)

    def relay_last():
        for h in range(NH):
            relay(2, h)

    steps = {"P": pool_in, "X": gram_x, "Y": gram_y, "F": far_in, "Z": gram_z, "A": gram_back,
             "R": lambda: [raw_in(h) for h in range(NH)], "L": relay_near, "M": relay_last,
             "0": lambda: relay(0, 0), "1": lambda: relay(1, 0)}
    shipped = 0
    for do in PLAN:
        if isinstance(do, int):
            ship(shipped, do)
            shipped = do
        else:
            steps[do]()

    for n, e in enumerate(near):
        arrived(slots.at[e], sn.at[n], rs.at[0, e])
    for i, o in enumerate(FAR):
        for k, p in enumerate(x_peers):
            slot = lax.rem(z + o, NZ) * NX + p
            for h in range(NH):
                arrived(slots.at[slot, rows(h), :], sx.at[i, h, k], rs.at[h, slot])

    def gather_core():
        for p in y_peers:
            arrived(gram.at[c, :, p], bs.at[p], br.at[p])
        send(gram.at[c], gram.at[c], es.at[0], er.at[0], other)

    def finish():
        arrived(gram.at[1 - c], es.at[0], er.at[0])
        for copy in started:
            copy.wait_send()

    return gather_core, finish


def kernel(send_h, route_h, slot_h, items_h, conf_h, out, send_v, route_v, send_s, route_s, slot_s, items, conf,
           slots, gram, sends_v, routes_v, sends_s, routes_s, pool, out1, out2, out3, out4, part, gc, sc, gx,
           s2, g2, s3, g3, s4, pan, pant, gh, gl, res, dirn, rr, gv, *rest):
    raw = [rest[NH * i : NH * i + NH] for i in range(3)]
    pools = [rest[NH * (3 + i) : NH * (4 + i)] for i in range(3)]
    ins, sems = rest[6 * NH], rest[6 * NH + 1 :]
    pairs = ((send_h, send_s), (route_h, route_s), (items_h, items), (send_h, send_v), (route_h, route_v),
             (slot_h, slot_s), (conf_h, conf))
    loads = [pltpu.make_async_copy(a, b, ins.at[i]) for i, (a, b) in enumerate(pairs)]
    for copy in loads:
        copy.start()

    def ready():
        for copy in loads[:5]:
            copy.wait()

    gather_core, finish = exchange(
        send_v, route_v, send_s, route_s, items, slots, gram, raw, sends_v, routes_v, sends_s, routes_s,
        pool, pools, out1, out2, out3, out4, part, gc, sc, gx, s2, g2, s3, g3, s4, *sems, ready)
    loads[5].wait()
    gather_panels(slot_s, slots, pan, pant)
    gather_core()
    loads[6].wait()
    right_side(conf, out, pan, res, dirn, rr)
    finish()
    solve(gram, conf, out, pan, pant, gh, gl, res, dirn, rr, gv)


def half_sweep(send_list, route_list, tile_slot, items, conf):
    dma = pltpu.SemaphoreType.DMA
    hbm = pl.BlockSpec(memory_space=pl.ANY)
    panel = (BLOCK, RANK)
    users = UB * BLOCK
    return pl.pallas_call(
        kernel,
        out_shape=jax.ShapeDtypeStruct((users, RANK), F32),
        in_specs=[hbm] * 5,
        out_specs=pl.BlockSpec(memory_space=pltpu.VMEM),
        scratch_shapes=[
            pltpu.VMEM((1, NG), jnp.int32), pltpu.VMEM((1, ND), jnp.int32),
            pltpu.SMEM((1, NG), jnp.int32), pltpu.SMEM((1, ND), jnp.int32), pltpu.SMEM((1, UB * TP), jnp.int32),
            pltpu.VMEM((PANELS_DEV, *panel), BF), pltpu.VMEM((UB * TP, BLOCK, BLOCK), BF),
            pltpu.VMEM((ND, *panel), BF), pltpu.VMEM((NC, NX, NY, 8, RANK), F32),
            pltpu.VMEM((3, 1, NG), jnp.int32), pltpu.VMEM((3, 1, ND), jnp.int32),
            pltpu.SMEM((3, 1, NG), jnp.int32), pltpu.SMEM((3, 1, ND), jnp.int32),
            pltpu.VMEM((NG, *panel), BF), pltpu.VMEM((NG, *panel), BF),
            pltpu.VMEM((len(NEAR), *panel), BF), pltpu.VMEM((3, NH, NX - 1, HB, RANK), BF),
            pltpu.VMEM((3, NH, NG, HB, RANK), BF),
            pltpu.VMEM((RANK, RANK), F32), pltpu.VMEM((128, RANK), F32),
            pltpu.VMEM((NY, 32, RANK), F32), pltpu.VMEM((NY, 32, RANK), F32),
            pltpu.VMEM((NX, 8, RANK), F32), pltpu.VMEM((NX, 8, RANK), F32),
            pltpu.VMEM((8, RANK), F32), pltpu.VMEM((NZ, 8, RANK), F32), pltpu.VMEM((NX, 8, RANK), F32),
            pltpu.VMEM((UB * TP * BLOCK, RANK), BF), pltpu.VMEM((UB * TP * BLOCK, RANK), BF),
            pltpu.VMEM((RANK, RANK), BF), pltpu.VMEM((RANK, RANK), BF),
            pltpu.VMEM((users, RANK), F32), pltpu.VMEM((users, RANK), F32), pltpu.VMEM((users, 128), F32),
            pltpu.VMEM((users, RANK), F32),
            *[pltpu.VMEM((PANELS_DEV, HB, RANK), BF)] * (3 * NH),
            *[pltpu.VMEM((NG, HB, RANK), BF)] * (3 * NH),
            dma((7,)),
            dma((2, 3)), dma((2, 3)), dma((2, 3)),
            dma((NH, 4)), dma((NH, 4)),
            dma((NG,)), dma((NG,)), dma((3, NH, NG)), dma((3, NH, NG)),
            dma((len(NEAR),)), dma((NH, ND)), dma((3, NH, NX - 1)),
            dma((1,)), dma((1,)), dma((NY,)), dma((NY,)), dma((NX,)), dma((NX,)), dma((NZ,)), dma((NZ,)),
            dma((NX,)), dma((NX,)), dma((NY,)), dma((NY,)), dma((1,)), dma((1,)),
        ],
        name="half_sweep",
        compiler_params=pltpu.CompilerParams(collective_id=0, has_side_effects=True, vmem_limit_bytes=54000 << 10),
    )(*[pltpu.with_memory_space_constraint(a, pltpu.HBM) for a in (send_list, route_list, tile_slot, items, conf)])


def shards(item_factors, send_list, route_list, tile_slot, confidence):
    return half_sweep(
        send_list.reshape(1, -1), route_list.reshape(1, -1), tile_slot,
        item_factors.reshape(-1, BLOCK, RANK), confidence,
    )


def solution(mesh):
    placed = (
        P(("grp", "dev"), None),
        P(("grp", "dev"), None, None),
        P(("grp", "dev"), None, None),
        P(("grp", "dev"), None),
        P(("grp", "dev"), None, None),
    )
    return jax.shard_map(
        shards, mesh=mesh, in_specs=placed, out_specs=P(("grp", "dev"), None), check_vma=False
    )
```

```python
import functools

import jax
import jax.numpy as jnp
from jax import lax
from jax.experimental import pallas as pl
from jax.experimental.pallas import tpu as pltpu
from jax.sharding import PartitionSpec as P

PANELS_DEV = 2
RANK = 256
BLOCK = 128
UB = 4
TP = 16
ITERS = 8
RIDGE = 0.1
NG, NY, NC, NX, NZ = 8, 4, 2, 4, 8
ND = NX * NZ
F32 = jnp.float32
BF = jnp.bfloat16
MESH = pl.DeviceIdType.MESH
FAR = (3, 5, 4)
NEAR = tuple((dz, dx) for dz in (2, 6, 1, 7, 0) for dx in (2, 1, 3, 0) if (dz, dx) != (0, 0))
NH = 1
HB = BLOCK // NH
PLAN = ("X", "P", "Y", "R", 19, "F", "Z", "L", "A", "M")
CHUNK = 1024
PER = CHUNK // BLOCK
WIDE = True


def dot(a, b):
    return jnp.dot(a, b, preferred_element_type=F32)


def half(ref, i):
    return ref.at[pl.ds(pl.multiple_of(i * 128, 128), 128), :]


def confs(conf, b, c):
    return jnp.concatenate([conf[b * TP + c * PER + j] for j in range(PER)], axis=1).astype(F32)


def chunk(b, c):
    first = (b * TP + c * PER) * BLOCK
    return slice(first, first + CHUNK)


def gather_panels(slot_s, slots, turned, pan, pant):
    def gather(t, carry):
        for k in range(2):
            slot = slot_s[0, 2 * t + k]
            pan[pl.ds(pl.multiple_of(t * RANK + k * BLOCK, BLOCK), BLOCK), :] = slots[slot]
            pant[pl.ds(pl.multiple_of(t * RANK, RANK), RANK), k * BLOCK : k * BLOCK + BLOCK] = turned[slot]
        return carry

    lax.fori_loop(0, UB * TP // 2, gather, 0, unroll=2)


def right_side(conf, out, pan, res, dirn, rr):
    for b in range(UB):
        acc = None
        for c in range(TP // PER):
            w = confs(conf, b, c)
            d = dot(jnp.where(w > 0, 1.0 + w, 0.0).astype(BF), pan[chunk(b, c), :])
            acc = d if acc is None else acc + d
        us = slice(b * BLOCK, (b + 1) * BLOCK)
        res[us, :] = acc
        dirn[us, :] = acc
        out[us, :] = jnp.zeros_like(acc)
        rr[us, :] = jnp.broadcast_to(jnp.sum(acc * acc, axis=1, keepdims=True), (BLOCK, 128))


def solve(gram, conf, out, pan, pant, gh, gl, res, dirn, rr, gv):
    g = gram[...].reshape(RANK, RANK)
    high = g.astype(BF)
    gh[...] = high
    gl[...] = (g - high.astype(F32)).astype(BF)

    def step(i, carry):
        if WIDE:
            v = dirn[...]
            vb = v.astype(BF)
            vl = (v - vb.astype(F32)).astype(BF)
            gv[...] = dot(vb, gh[...]) + dot(vb, gl[...])
        for b in range(UB):
            us = slice(b * BLOCK, (b + 1) * BLOCK)
            v = dirn[us, :]
            vb = v.astype(BF)
            if WIDE:
                acc = gv[us, :] + RIDGE * v
            else:
                vl = (v - vb.astype(F32)).astype(BF)
                acc = dot(vb, gh[...]) + dot(vb, gl[...]) + dot(vl, gh[...]) + RIDGE * v
            for c in range(TP // PER):
                first = (b * TP + c * PER) * BLOCK
                s = jnp.concatenate(
                    [dot(vb, pant[first + 256 * j : first + 256 * j + 256, :]) for j in range(PER // 2)], axis=1
                )
                acc = acc + dot((confs(conf, b, c) * s).astype(BF), pan[chunk(b, c), :])
            old = rr[us, 0:1]
            alpha = old / jnp.sum(v * acc, axis=1, keepdims=True)
            out[us, :] = out[us, :] + alpha * v
            r = res[us, :] - alpha * acc
            new = jnp.sum(r * r, axis=1, keepdims=True)
            res[us, :] = r
            dirn[us, :] = r + (new / old) * v
            rr[us, :] = jnp.broadcast_to(new, (BLOCK, 128))
        return carry

    lax.fori_loop(0, ITERS, step, 0)


def exchange(send_v, route_v, send_s, route_s, items, slots, turned, gram, raw, sends_v, routes_v, sends_s, routes_s,
             pool, pools, out1, out2, out3, out4, part, gc, sc, gx, s2, g2, s3, g3, s4,
             local, sm, rm, sr, rr, sp, rp, sq, rq, sn, rs, sx,
             cs, cr, ys, yr, xs, xr, zs, zr, as_, ar, bs, br, es, er, before_wait):
    g = lax.axis_index("grp")
    d = lax.axis_index("dev")
    z, x = d // NX, lax.rem(d, NX)
    y, c = g // NC, lax.rem(g, NC)
    grp_peers = [lax.rem(g + k, NG) for k in (1, 3, 5, 7, 2, 6, 4)]
    x_peers = [lax.rem(x + k, NX) for k in range(1, NX)]
    y_peers = [lax.rem(y + k, NY) for k in range(1, NY)]
    z_peers = [lax.rem(z + k, NZ) for k in range(1, NZ)]

    def at_z(k):
        return {"dev": lax.rem(z + k, NZ) * NX + x}

    def at_x(p):
        return {"dev": z * NX + p}

    def at_y(p):
        return {"grp": p * NC + c}

    other = {"grp": y * NC + 1 - c}

    barrier = pltpu.get_barrier_semaphore()
    near = [lax.rem(z + dz, NZ) * NX + lax.rem(x + dx, NX) for dz, dx in NEAR]
    for p in grp_peers:
        pl.semaphore_signal(barrier, inc=1, device_id={"grp": p}, device_id_type=MESH)
    for e in near:
        pl.semaphore_signal(barrier, inc=1, device_id={"dev": e}, device_id_type=MESH)
    for o in FAR:
        pl.semaphore_signal(barrier, inc=1, device_id=at_z(o), device_id_type=MESH)

    started = []

    def send(src, dst, ss, rs_, where):
        copy = pltpu.make_async_remote_copy(
            src_ref=src, dst_ref=dst, send_sem=ss, recv_sem=rs_, device_id=where, device_id_type=MESH
        )
        copy.start()
        started.append(copy)

    def arrived(ref, ss, rs_):
        pltpu.make_async_remote_copy(
            src_ref=ref, dst_ref=ref, send_sem=ss, recv_sem=rs_, device_id=other, device_id_type=MESH
        ).wait_recv()

    before_wait()
    flat = items[...].reshape(PANELS_DEV * BLOCK, RANK)
    part[...] = lax.dot_general(flat, flat, (((0,), (0,)), ((), ())), preferred_element_type=F32)
    for j in range(NG):
        out1[j] = items[send_s[0, j]]
    pool[g] = out1[g]
    pl.semaphore_wait(barrier, len(grp_peers) + len(near) + len(FAR))

    for i, o in enumerate(FAR):
        send(send_v, sends_v.at[i], sm.at[0, i], rm.at[0, i], at_z(NZ - o))
        send(route_v, routes_v.at[i], sm.at[1, i], rm.at[1, i], at_z(NZ - o))
    def rows(h):
        return slice(h * HB, h * HB + HB)

    def send_raw(h):
        for i in range(2):
            send(items.at[:, rows(h), :], raw[i][h], sr.at[h, i], rr.at[h, i], at_z(NZ - FAR[i]))

    send_raw(0)
    for p in grp_peers:
        send(out1.at[p], pool.at[g], sp.at[p], rp.at[g], {"grp": p})
    for h in range(1, NH):
        send_raw(h)
    send(half(part, 1 - c), gc, cs.at[0], cr.at[0], other)
    arrived(gc, cs.at[0], cr.at[0])
    sc[...] = (half(part, c)[...] + gc[...]).reshape(NX, 32, RANK)
    gx[x] = sc[x]
    for p in x_peers:
        send(sc.at[p], gx.at[x], xs.at[p], xr.at[x], at_x(p))

    def fill(n):
        if n < len(near):
            out2[n] = pool[route_s[0, near[n]]]

    def ship(first, last):
        for n in range(first, last):
            fill(n + 2)
            send(out2.at[n], slots.at[d], sn.at[n], rs.at[0, d], {"dev": near[n]})

    def proxy(i, h):
        for j in range(NG):
            out4[i, h, j] = raw[i][h][sends_s[i, 0, j]]
        pools[i][h][g] = out4[i, h, g]
        for p in grp_peers:
            send(out4.at[i, h, p], pools[i][h].at[g], sq.at[i, h, p], rq.at[i, h, g], {"grp": p})

    for i in range(3):
        arrived(sends_v.at[i], sm.at[0, i], rm.at[0, i])
        pltpu.make_async_copy(sends_v.at[i], sends_s.at[i], local.at[0, i]).start()
        arrived(routes_v.at[i], sm.at[1, i], rm.at[1, i])
        pltpu.make_async_copy(routes_v.at[i], routes_s.at[i], local.at[1, i]).start()
    for i in range(3):
        pltpu.make_async_copy(sends_v.at[i], sends_s.at[i], local.at[0, i]).wait()
        pltpu.make_async_copy(routes_v.at[i], routes_s.at[i], local.at[1, i]).wait()

    def raw_in(h):
        arrived(raw[0][h], sr.at[h, 0], rr.at[h, 0])
        send(raw[0][h].at[1], raw[2][h].at[1], sr.at[h, 3], rr.at[h, 3], at_z(NZ - 1))
        arrived(raw[1][h], sr.at[h, 1], rr.at[h, 1])
        send(raw[1][h].at[0], raw[2][h].at[0], sr.at[h, 2], rr.at[h, 2], at_z(1))
        proxy(0, h)
        proxy(1, h)

    def relay(i, h):
        slot = lax.rem(z + FAR[i], NZ) * NX + x
        for p in grp_peers:
            arrived(pools[i][h].at[p], sq.at[i, h, p], rq.at[i, h, p])
        for k, p in enumerate(x_peers):
            out3[i, h, k] = pools[i][h][routes_s[i, 0, z * NX + p]]
        for k, p in enumerate(x_peers):
            send(out3.at[i, h, k], slots.at[slot, rows(h), :], sx.at[i, h, k], rs.at[h, slot], at_x(p))
        slots[slot, rows(h), :] = pools[i][h][routes_s[i, 0, d]]

    def pool_in():
        for p in grp_peers:
            arrived(pool.at[p], sp.at[p], rp.at[p])
        fill(0)
        fill(1)
        slots[d] = pool[route_s[0, d]]

    def gram_x():
        for p in x_peers:
            arrived(gx.at[p], xs.at[p], xr.at[p])
        s2[...] = ((gx[0] + gx[1]) + (gx[2] + gx[3])).reshape(NY, 8, RANK)
        g2[y] = s2[y]
        for p in y_peers:
            send(s2.at[p], g2.at[y], ys.at[p], yr.at[y], at_y(p))

    def gram_y():
        for p in y_peers:
            arrived(g2.at[p], ys.at[p], yr.at[p])
        s3[...] = (g2[0] + g2[1]) + (g2[2] + g2[3])
        g3[z] = s3[...]
        for k, p in enumerate(z_peers):
            send(s3, g3.at[z], zs.at[p], zr.at[z], at_z(k + 1))

    def far_in():
        for h in range(NH):
            arrived(raw[2][h].at[0], sr.at[h, 2], rr.at[h, 2])
            arrived(raw[2][h].at[1], sr.at[h, 3], rr.at[h, 3])
            proxy(2, h)

    def gram_z():
        for p in z_peers:
            arrived(g3.at[p], zs.at[p], zr.at[p])
        s4[x] = ((g3[0] + g3[1]) + (g3[2] + g3[3])) + ((g3[4] + g3[5]) + (g3[6] + g3[7]))
        for p in x_peers:
            send(s4.at[x], s4.at[x], as_.at[p], ar.at[x], at_x(p))

    def gram_back():
        for p in x_peers:
            arrived(s4.at[p], as_.at[p], ar.at[p])
        gram[c, :, y] = s4[...]
        for p in y_peers:
            send(s4, gram.at[c, :, y], bs.at[p], br.at[y], at_y(p))

    def relay_near():
        for h in range(NH):
            relay(0, h)
            relay(1, h)

    def relay_last():
        for h in range(NH):
            relay(2, h)

    steps = {"P": pool_in, "X": gram_x, "Y": gram_y, "F": far_in, "Z": gram_z, "A": gram_back,
             "R": lambda: [raw_in(h) for h in range(NH)], "L": relay_near, "M": relay_last,
             "0": lambda: relay(0, 0), "1": lambda: relay(1, 0)}
    shipped = 0
    for do in PLAN:
        if isinstance(do, int):
            ship(shipped, do)
            shipped = do
        else:
            steps[do]()

    for n, e in enumerate(near):
        arrived(slots.at[e], sn.at[n], rs.at[0, e])
        turned[e] = slots[e].T
    turned[d] = slots[d].T
    for i, o in enumerate(FAR):
        for k, p in enumerate(x_peers):
            slot = lax.rem(z + o, NZ) * NX + p
            for h in range(NH):
                arrived(slots.at[slot, rows(h), :], sx.at[i, h, k], rs.at[h, slot])
            turned[slot] = slots[slot].T
        slot = lax.rem(z + o, NZ) * NX + x
        turned[slot] = slots[slot].T

    def gather_core():
        for p in y_peers:
            arrived(gram.at[c, :, p], bs.at[p], br.at[p])
        send(gram.at[c], gram.at[c], es.at[0], er.at[0], other)

    def finish():
        arrived(gram.at[1 - c], es.at[0], er.at[0])
        for copy in started:
            copy.wait_send()

    return gather_core, finish


def kernel(send_h, route_h, slot_h, items_h, conf_h, out, send_v, route_v, send_s, route_s, slot_s, items, conf,
           slots, turned, gram, sends_v, routes_v, sends_s, routes_s, pool, out1, out2, out3, out4, part, gc, sc, gx,
           s2, g2, s3, g3, s4, pan, pant, gh, gl, res, dirn, rr, gv, *rest):
    raw = [rest[NH * i : NH * i + NH] for i in range(3)]
    pools = [rest[NH * (3 + i) : NH * (4 + i)] for i in range(3)]
    ins, sems = rest[6 * NH], rest[6 * NH + 1 :]
    pairs = ((send_h, send_s), (route_h, route_s), (items_h, items), (send_h, send_v), (route_h, route_v),
             (slot_h, slot_s), (conf_h, conf))
    loads = [pltpu.make_async_copy(a, b, ins.at[i]) for i, (a, b) in enumerate(pairs)]
    for copy in loads:
        copy.start()

    def ready():
        for copy in loads[:5]:
            copy.wait()

    gather_core, finish = exchange(
        send_v, route_v, send_s, route_s, items, slots, turned, gram, raw, sends_v, routes_v, sends_s, routes_s,
        pool, pools, out1, out2, out3, out4, part, gc, sc, gx, s2, g2, s3, g3, s4, *sems, ready)
    loads[5].wait()
    gather_panels(slot_s, slots, turned, pan, pant)
    gather_core()
    loads[6].wait()
    right_side(conf, out, pan, res, dirn, rr)
    finish()
    solve(gram, conf, out, pan, pant, gh, gl, res, dirn, rr, gv)


def half_sweep(send_list, route_list, tile_slot, items, conf):
    dma = pltpu.SemaphoreType.DMA
    hbm = pl.BlockSpec(memory_space=pl.ANY)
    panel = (BLOCK, RANK)
    users = UB * BLOCK
    return pl.pallas_call(
        kernel,
        out_shape=jax.ShapeDtypeStruct((users, RANK), F32),
        in_specs=[hbm] * 5,
        out_specs=pl.BlockSpec(memory_space=pltpu.VMEM),
        scratch_shapes=[
            pltpu.VMEM((1, NG), jnp.int32), pltpu.VMEM((1, ND), jnp.int32),
            pltpu.SMEM((1, NG), jnp.int32), pltpu.SMEM((1, ND), jnp.int32), pltpu.SMEM((1, UB * TP), jnp.int32),
            pltpu.VMEM((PANELS_DEV, *panel), BF), pltpu.VMEM((UB * TP, BLOCK, BLOCK), BF),
            pltpu.VMEM((ND, *panel), BF), pltpu.VMEM((ND, RANK, BLOCK), BF), pltpu.VMEM((NC, NX, NY, 8, RANK), F32),
            pltpu.VMEM((3, 1, NG), jnp.int32), pltpu.VMEM((3, 1, ND), jnp.int32),
            pltpu.SMEM((3, 1, NG), jnp.int32), pltpu.SMEM((3, 1, ND), jnp.int32),
            pltpu.VMEM((NG, *panel), BF), pltpu.VMEM((NG, *panel), BF),
            pltpu.VMEM((len(NEAR), *panel), BF), pltpu.VMEM((3, NH, NX - 1, HB, RANK), BF),
            pltpu.VMEM((3, NH, NG, HB, RANK), BF),
            pltpu.VMEM((RANK, RANK), F32), pltpu.VMEM((128, RANK), F32),
            pltpu.VMEM((NY, 32, RANK), F32), pltpu.VMEM((NY, 32, RANK), F32),
            pltpu.VMEM((NX, 8, RANK), F32), pltpu.VMEM((NX, 8, RANK), F32),
            pltpu.VMEM((8, RANK), F32), pltpu.VMEM((NZ, 8, RANK), F32), pltpu.VMEM((NX, 8, RANK), F32),
            pltpu.VMEM((UB * TP * BLOCK, RANK), BF), pltpu.VMEM((UB * TP * BLOCK, RANK), BF),
            pltpu.VMEM((RANK, RANK), BF), pltpu.VMEM((RANK, RANK), BF),
            pltpu.VMEM((users, RANK), F32), pltpu.VMEM((users, RANK), F32), pltpu.VMEM((users, 128), F32),
            pltpu.VMEM((users, RANK), F32),
            *[pltpu.VMEM((PANELS_DEV, HB, RANK), BF)] * (3 * NH),
            *[pltpu.VMEM((NG, HB, RANK), BF)] * (3 * NH),
            dma((7,)),
            dma((2, 3)), dma((2, 3)), dma((2, 3)),
            dma((NH, 4)), dma((NH, 4)),
            dma((NG,)), dma((NG,)), dma((3, NH, NG)), dma((3, NH, NG)),
            dma((len(NEAR),)), dma((NH, ND)), dma((3, NH, NX - 1)),
            dma((1,)), dma((1,)), dma((NY,)), dma((NY,)), dma((NX,)), dma((NX,)), dma((NZ,)), dma((NZ,)),
            dma((NX,)), dma((NX,)), dma((NY,)), dma((NY,)), dma((1,)), dma((1,)),
        ],
        name="half_sweep",
        compiler_params=pltpu.CompilerParams(collective_id=0, has_side_effects=True, vmem_limit_bytes=54000 << 10),
    )(*[pltpu.with_memory_space_constraint(a, pltpu.HBM) for a in (send_list, route_list, tile_slot, items, conf)])


def shards(item_factors, send_list, route_list, tile_slot, confidence):
    return half_sweep(
        send_list.reshape(1, -1), route_list.reshape(1, -1), tile_slot,
        item_factors.reshape(-1, BLOCK, RANK), confidence,
    )


def solution(mesh):
    placed = (
        P(("grp", "dev"), None),
        P(("grp", "dev"), None, None),
        P(("grp", "dev"), None, None),
        P(("grp", "dev"), None),
        P(("grp", "dev"), None, None),
    )
    return jax.shard_map(
        shards, mesh=mesh, in_specs=placed, out_specs=P(("grp", "dev"), None), check_vma=False
    )
```
